32 devices in a mesh: row: 4 (over z), col: 4 (over y, core), occ: 2 (over x).
Axes of the slice: x: 2, y: 2, z: 4, core: 2. Of those that a mesh axis runs over, the one named last changes fastest.
Arguments:
- doubles: float32 [4, 2048, 4, 2048], P(None, 'row', 'occ', 'col'), may hold values from -6 to 6
- cycle: float32 [4, 2048, 4, 2048], P('occ', 'row', None, 'col'), may hold values from -0.0625 to 0.0625
- occ_energy: float32 [4], replicated, may hold values from -3 to -0.5
- virt_energy: float32 [2048], replicated, may hold values from 0.5 to 3
- orbital_irrep: int32 [2052], replicated, may hold values from 0 to 3
Outputs:
- update: float32 [4, 2048, 4, 2048], P(None, 'row', 'occ', 'col')
The draws below stay inside these ranges and needn't reach their ends.
Inputs may be any that keep to these rules, and one draw needn't show every extreme that they name: `orbital_irrep`: C2v irrep labels; the product of two irreps is the bitwise xor of their labels.
All inputs are finite; a program needn't handle non-finite values.
Results may differ from the reference program's by a relative error of at most 0.00007.
Values sent between devices are 32-bit elements; how exact they have to be, the bound alone decides.
No kernel may reach another device: no remote copies, remote signals or barrier semaphores. Data moves between devices by JAX's collectives and lax.ppermute only.
A program may use at most 192 MiB of HBM per device.

```python
import jax
import jax.numpy as jnp
from jax import lax

V = 2048
NO = 4
NK = 4


def with_ends(result, key, low, high):
    extent = result.shape
    place = [jax.random.randint(jax.random.fold_in(key, axis), (), 0, extent[axis]) for axis in range(len(extent))]
    result = result.at[tuple(place)].set(low)
    longest = extent.index(max(extent))
    place[longest] = (place[longest] + 1) % extent[longest]
    return result.at[tuple(place)].set(high)


def level_of(key, shape, shards, low, top_value):
    loudness = 1.0
    for axis_at, blocks in shards:
        heights = jax.random.uniform(jax.random.fold_in(jax.random.fold_in(key, 6), axis_at), (blocks,), jnp.float32, low / len(shards), top_value / len(shards))
        loudness = loudness * jnp.repeat(jnp.exp(heights), shape[axis_at] // blocks).reshape((-1,) + (1,) * (len(shape) - 1 - axis_at))
    return loudness


def bell_draw(rng, extent, deviation, reach, pieces=(), dtype=jnp.bfloat16):
    result = deviation * jax.random.normal(rng, extent, jnp.float32)
    if pieces:
        result = result * level_of(rng, extent, pieces, -0.22, 0.18)
    return jnp.clip(result, -reach, reach).astype(dtype)


def setup_inputs(seed: int = 0) -> dict:
    seeds = jax.random.split(jax.random.key(seed), 6)
    return {
        "doubles": bell_draw(seeds[0], (NO, V, NK, V), 1.0, 6.0, ((1, 4), (2, 2), (3, 4)), jnp.float32),
        "cycle": bell_draw(seeds[1], (NK, V, NO, V), (NK * V) ** -0.5, 0.0625, ((0, 2), (1, 4), (3, 4)), jnp.float32),
        "occ_energy": jnp.clip(jax.random.uniform(seeds[2], (NO,), jnp.float32, -3.0, -0.5), -3.0, -0.5),
        "virt_energy": jnp.clip(jax.random.uniform(seeds[3], (V,), jnp.float32, 0.5, 3.0), 0.5, 3.0),
        "orbital_irrep": with_ends(jax.random.randint(seeds[4], (NO + V,), 0, 4), jax.random.fold_in(seeds[4], 1), 0, 3).astype(jnp.int32),
    }


def reference(doubles, cycle, occ_energy, virt_energy, orbital_irrep):
    occ_irrep = orbital_irrep[:NO]
    virt_irrep = orbital_irrep[NO:]
    left = doubles.reshape(NO * V, NK * V)
    right = cycle.reshape(NK * V, NO * V)
    cycle_sum = jnp.dot(left, right, precision=lax.Precision.HIGHEST, preferred_element_type=jnp.float32)
    cycle_sum = cycle_sum.reshape(NO, V, NO, V)
    paired = cycle_sum + jnp.transpose(cycle_sum, (2, 3, 0, 1))
    denom = (virt_energy[None, :, None, None] + virt_energy[None, None, None, :]
             - occ_energy[:, None, None, None] - occ_energy[None, None, :, None])
    sector = jnp.bitwise_xor(jnp.bitwise_xor(occ_irrep[:, None, None, None], virt_irrep[None, :, None, None]),
                             jnp.bitwise_xor(occ_irrep[None, None, :, None], virt_irrep[None, None, None, :]))
    return jnp.where(sector == 0, paired / denom, jnp.zeros_like(paired))
```

```python
import functools

import jax
import jax.numpy as jnp
from jax import lax
from jax.experimental import pallas as pl
from jax.experimental.pallas import tpu as pltpu
from jax.sharding import PartitionSpec as P

N_IRREPS = 4
VMEM_LIMIT = 56 * 1024 * 1024


def split(x):
    high = x.astype(jnp.bfloat16)
    low = (x - high.astype(jnp.float32)).astype(jnp.bfloat16)
    return high, low


def dot(a, b, contract=((1,), (0,))):
    return lax.dot_general(a, b, (contract, ((), ())), preferred_element_type=jnp.float32)


def sort_body(place_ref, rows_ref, out_ref):
    tile_a, depth = rows_ref.shape[1:]
    chunks, n_piece, _, sub, _ = out_ref.shape[1:]
    places = lax.broadcasted_iota(jnp.int32, (tile_a, tile_a), 0)
    order = (place_ref[...] == places).astype(jnp.float32).astype(jnp.bfloat16)
    high, low = split(rows_ref[0])
    value = dot(order, high) + dot(order, low)
    out_ref[0, :, :, 0] = value.reshape(chunks, n_piece, sub, depth)


def sort_rows(doubles, place, n_occ, chunks, n):
    n_i, tile_a, k_half, tile_c = doubles.shape
    half, sub = n_i // n_occ, tile_a // (chunks * n)
    shape = (half, chunks, n, n_occ, sub, k_half * tile_c)
    return pl.pallas_call(
        sort_body,
        out_shape=jax.ShapeDtypeStruct(shape, jnp.float32),
        grid=(half, n_occ),
        in_specs=[
            pl.BlockSpec((1, tile_a), lambda m, o: (0, 0)),
            pl.BlockSpec((1, tile_a, k_half * tile_c), lambda m, o: (o * half + m, 0, 0)),
        ],
        out_specs=pl.BlockSpec((1, chunks, n, 1, sub, k_half * tile_c), lambda m, o: (m, 0, 0, o, 0, 0)),
        compiler_params=pltpu.CompilerParams(vmem_limit_bytes=VMEM_LIMIT),
        cost_estimate=pl.CostEstimate(
            flops=4 * doubles.size * tile_a, bytes_accessed=8 * doubles.size, transcendentals=0
        ),
    )(place, doubles.reshape(n_i, tile_a, k_half * tile_c))


def compact_body(cap, key_ref, right_ref, high_ref, low_ref, select_ref, both_ref):
    n_j, tile_b = select_ref.shape[:2]
    width = N_IRREPS * cap

    @pl.when(pl.program_id(0) == 0)
    def _():
        for j in range(n_j):
            slots = lax.broadcasted_iota(jnp.int32, (tile_b, width), 1)
            select_ref[j] = (key_ref[j] == slots).astype(jnp.float32).astype(jnp.bfloat16)

    rows = right_ref.shape[0]
    for j in range(n_j):
        high, low = split(right_ref[:, j * tile_b : (j + 1) * tile_b])
        both_ref[j, :rows] = high
        both_ref[j, rows:] = low

    @pl.loop(0, N_IRREPS)
    def _(q):
        span = pl.ds(pl.multiple_of(q * cap, 128), cap)
        total = dot(both_ref[0], select_ref[0, :, span])
        for j in range(1, n_j):
            total += dot(both_ref[j], select_ref[j, :, span])
        high_ref[:, span] = total[:rows].astype(jnp.bfloat16)
        low_ref[:, span] = total[rows:].astype(jnp.bfloat16)


def compact(right, key, cap):
    k_half, tile_c, n_j, tile_b = right.shape
    step = min(tile_c, 256)
    width = N_IRREPS * cap
    out = jax.ShapeDtypeStruct((k_half * tile_c, width), jnp.bfloat16)
    return pl.pallas_call(
        functools.partial(compact_body, cap),
        out_shape=(out, out),
        grid=(k_half * tile_c // step,),
        in_specs=[
            pl.BlockSpec((n_j, tile_b, 1), lambda s: (0, 0, 0)),
            pl.BlockSpec((step, n_j * tile_b), lambda s: (s, 0)),
        ],
        out_specs=[pl.BlockSpec((step, width), lambda s: (s, 0))] * 2,
        scratch_shapes=[
            pltpu.VMEM((n_j, tile_b, width), jnp.bfloat16),
            pltpu.VMEM((n_j, 2 * step, tile_b), jnp.bfloat16),
        ],
        compiler_params=pltpu.CompilerParams(vmem_limit_bytes=VMEM_LIMIT),
        cost_estimate=pl.CostEstimate(
            flops=4 * k_half * tile_c * n_j * tile_b * width, bytes_accessed=4 * right.size, transcendentals=0
        ),
    )(key, right.reshape(k_half * tile_c, n_j * tile_b))


def product_body(cap, scalar_ref, irrep_ref, near_ref, far_ref, high_ref, low_ref, out_ref, *scratch):
    left_high_ref, left_low_ref = scratch
    n_row, _, sub, depth = near_ref.shape[1:]
    row_pos, col_pos, row_i = scalar_ref[1], scalar_ref[2], scalar_ref[3]
    for at, ref in enumerate((near_ref, far_ref)):
        left_high_ref[at], left_low_ref[at] = split(ref[0, :, 0].reshape(n_row * sub, depth))
    out_ref[...] = jnp.zeros_like(out_ref)

    @pl.loop(0, 2 * N_IRREPS)
    def _(step):
        at, irrep = step // N_IRREPS, step % N_IRREPS
        place = jnp.bitwise_xor(col_pos, at) % 2
        piece = jnp.bitwise_xor(col_pos, 2 * pl.program_id(0) + at)

        @pl.when(scalar_ref[4 + piece * N_IRREPS + irrep] > 0)
        def _():
            span = pl.ds(pl.multiple_of(jnp.bitwise_xor(irrep, row_i) * cap, 128), cap)
            right_high = high_ref[:, span]
            left_high = left_high_ref[at]
            value = dot(left_low_ref[at], right_high) + dot(left_high, low_ref[:, span])
            value += dot(left_high, right_high)
            for t in range(n_row):
                r = jnp.bitwise_xor(row_pos, t)
                part = value[t * sub : (t + 1) * sub]
                out_ref[r, place] = jnp.where(irrep_ref[r, place] == irrep, part, out_ref[r, place])


def product(scalars, row_irrep, near, far, right_high, right_low, cap):
    n_pair, n_row, _, sub, depth = near.shape
    width = right_high.shape[1]
    pair = lambda v, scalars: (0, jnp.bitwise_xor(scalars[2] // 2, v), 0, 0)
    left = pl.BlockSpec((1, n_row, 1, sub, depth), lambda v, scalars: (v, 0, scalars[0], 0, 0))
    right = pl.BlockSpec((depth, width), lambda v, scalars: (0, 0), pipeline_mode=pl.Buffered(1))
    spec = pltpu.PrefetchScalarGridSpec(
        num_scalar_prefetch=1,
        grid=(n_pair,),
        in_specs=[pl.BlockSpec((n_row, 2, sub, 1), pair), left, left, right, right],
        out_specs=pl.BlockSpec((n_row, 2, sub, cap), pair),
        scratch_shapes=[pltpu.VMEM((2, n_row * sub, depth), jnp.bfloat16)] * 2,
    )
    rows = 2 * n_pair * n_row * sub
    return pl.pallas_call(
        functools.partial(product_body, cap),
        out_shape=jax.ShapeDtypeStruct((n_row, 2 * n_pair, sub, cap), jnp.float32),
        grid_spec=spec,
        compiler_params=pltpu.CompilerParams(vmem_limit_bytes=VMEM_LIMIT),
        cost_estimate=pl.CostEstimate(
            flops=3 * rows * depth * width, bytes_accessed=4 * rows * depth + 4 * depth * width, transcendentals=0
        ),
    )(scalars, row_irrep, near, far, right_high, right_low)


def finish_body(
    cap, occ_pos_ref, key_c_ref, slot_r_ref, irrep_i_ref, irrep_a_ref, place_a_ref, place_b_ref, irrep_jb_ref,
    energy_a_ref, energy_b_ref, energy_ij_ref, own_ref, swapped_ref, turned_ref, *refs,
):
    base_ref = refs[0] if len(refs) == 5 else None
    out_ref, expand_ref, turned_high_ref, turned_low_ref = refs[-4:]
    i = pl.program_id(0)
    half, tile_b = key_c_ref.shape
    tile_a = own_ref.shape[1]
    rows = out_ref.shape[1]

    def one_hot(column, length):
        hit = column == lax.broadcasted_iota(jnp.int32, (column.shape[0], length), 1)
        return hit.astype(jnp.float32).astype(jnp.bfloat16)

    @pl.when((i == 0) & (pl.program_id(1) == 0))
    def _():
        unsort = one_hot(place_b_ref[...], tile_b)
        slots = lax.broadcasted_iota(jnp.int32, (cap, tile_b), 0)
        for j in range(half):
            span = pl.ds(j * tile_b, tile_b)
            hit = key_c_ref[pl.ds(j, 1), :] == slots
            expand_ref[:, span] = hit.astype(jnp.float32).astype(jnp.bfloat16)
            high, low = split(turned_ref[j])
            turned_high_ref[span, :] = dot(unsort, high).astype(jnp.bfloat16)
            turned_low_ref[span, :] = dot(unsort, low).astype(jnp.bfloat16)

    mine = i // half == occ_pos_ref[0]
    unsort = one_hot(place_a_ref[...], tile_a)
    high, low = split(jnp.where(mine, own_ref[0], swapped_ref[0]))
    high, low = dot(unsort, high).astype(jnp.bfloat16), dot(unsort, low).astype(jnp.bfloat16)
    direct = dot(high, expand_ref[...]) + dot(low, expand_ref[...])
    pick = one_hot(slot_r_ref[0], cap)
    across = ((1,), (1,))
    turned = dot(pick, turned_high_ref[...], across) + dot(pick, turned_low_ref[...], across)
    paired = direct + turned
    row_class = jnp.bitwise_xor(irrep_a_ref[...], irrep_i_ref[i])
    for j in range(half):
        piece = paired[:, j * tile_b : (j + 1) * tile_b]
        denom = energy_a_ref[...] + energy_b_ref[...] - energy_ij_ref[i] - energy_ij_ref[2 * half + j]
        value = jnp.where(row_class == irrep_jb_ref[pl.ds(j, 1), :], piece / denom, jnp.zeros_like(piece))
        if base_ref is not None:
            value = value + base_ref[0, :, j, :]
        out_ref[0, :, j, :] = value


def finish(tables, own, swapped, turned, base, cap, shape):
    n_i, tile_a, half, tile_b = shape
    rows = min(tile_a, 256)
    block = pl.BlockSpec((1, rows, half, tile_b), lambda i, s: (i, s, 0, 0))
    part = pl.BlockSpec((1, tile_a, cap), lambda i, s: (i % half, 0, 0))
    smem = pl.BlockSpec(memory_space=pltpu.SMEM)
    whole = lambda x: pl.BlockSpec(x.shape, lambda i, s: (0,) * x.ndim)
    column = pl.BlockSpec((rows, 1), lambda i, s: (s, 0))
    occ_pos, key_c, slot_r, irrep_i, irrep_a, place_a, place_b, irrep_jb, energy_a, energy_b, energy_ij = tables
    args = list(tables) + [own, swapped, turned]
    specs = [
        smem, whole(key_c), pl.BlockSpec((1, rows, 1), lambda i, s: (i, s, 0)), smem, column, column, whole(place_b),
        whole(irrep_jb), column, whole(energy_b), smem, part, part, whole(turned),
    ]
    aliases = {}
    if base is not None:
        aliases = {len(args): 0}
        args.append(base)
        specs.append(block)
    return pl.pallas_call(
        functools.partial(finish_body, cap),
        out_shape=jax.ShapeDtypeStruct(shape, jnp.float32),
        grid=(n_i, tile_a // rows),
        in_specs=specs,
        out_specs=block,
        scratch_shapes=[
            pltpu.VMEM((cap, half * tile_b), jnp.bfloat16),
            pltpu.VMEM((half * tile_b, cap), jnp.bfloat16),
            pltpu.VMEM((half * tile_b, cap), jnp.bfloat16),
        ],
        input_output_aliases=aliases,
        compiler_params=pltpu.CompilerParams(vmem_limit_bytes=VMEM_LIMIT),
        cost_estimate=pl.CostEstimate(
            flops=8 * n_i * tile_a * cap * half * tile_b, bytes_accessed=4 * n_i * tile_a * (half * tile_b + cap),
            transcendentals=0,
        ),
    )(*args)


def after(x, *others):
    return lax.optimization_barrier((x,) + others)


def flipped(x, axis, n, bits):
    return lax.ppermute(x, axis, [(d, d ^ bits) for d in range(n)])


def exchange(pick, axis, n):
    return jnp.stack([pick(0)] + [flipped(pick(t), axis, n, t) for t in range(1, n)])


def turn(x, n):
    for axis in ("col", "row", "col"):
        x = lax.all_to_all(x, axis, split_axis=0, concat_axis=0, tiled=True)
    return x


def shards(doubles, cycle, occ_energy, virt_energy, orbital_irrep):
    n_i, tile_a, k_half, tile_c = doubles.shape
    n_j, tile_b = cycle.shape[2:]
    n, n_occ = lax.axis_size("row"), lax.axis_size("occ")
    half = n_j // n_occ
    columns = n_j * tile_b
    cap = min(columns, -(-columns * 5 // (N_IRREPS * 4 * 128)) * 128)
    chunks = 2 if tile_a % (16 * n) == 0 else 1
    sub = tile_a // (chunks * n)
    row_pos, col_pos, occ_pos = lax.axis_index("row"), lax.axis_index("col"), lax.axis_index("occ")
    occ_irrep, virt_irrep = orbital_irrep[:n_j], orbital_irrep[n_j:]

    blocks = virt_irrep.reshape(n, tile_b)
    kinds = jnp.arange(N_IRREPS, dtype=jnp.int32)
    counts = jnp.sum((blocks[:, None, :] == kinds[:, None]).astype(jnp.int32), axis=2)
    sizes = sum(counts[:, jnp.bitwise_xor(kinds, occ_irrep[j])] for j in range(n_j))
    rounds = (jnp.max(sizes) + cap - 1) // cap

    starts = jnp.cumsum(counts, axis=1) - counts

    def places(block_pos):
        irrep = lax.dynamic_index_in_dim(blocks, block_pos, 0, keepdims=False)
        count = lax.dynamic_index_in_dim(counts, block_pos, 0, keepdims=False)
        start = lax.dynamic_index_in_dim(starts, block_pos, 0, keepdims=False)
        order = jnp.arange(tile_b, dtype=jnp.int32)
        earlier = (irrep[:, None] == irrep[None, :]) & (order[:, None] < order[None, :])
        rank = jnp.sum(earlier.astype(jnp.int32), axis=0)
        look_up = lambda table, index: sum(jnp.where(index == g, table[g], 0) for g in range(N_IRREPS))
        slots = []
        for j in range(n_j):
            before = jnp.zeros((tile_b,), jnp.int32)
            for other in range(j):
                before += look_up(count, jnp.bitwise_xor(irrep, jnp.bitwise_xor(occ_irrep[j], occ_irrep[other])))
            slots.append(before + rank)
        return jnp.stack(slots), jnp.bitwise_xor(irrep[None, :], occ_irrep[:, None]), look_up(start, irrep) + rank

    slot_c, class_c, place_c = places(col_pos)
    slot_r, _, place_r = places(row_pos)

    order = jnp.arange(tile_a, dtype=jnp.int32)
    row_irrep = sum((order[None, :] >= starts[:, g, None]).astype(jnp.int32) for g in range(1, N_IRREPS))
    row_irrep = row_irrep.reshape(n, chunks, n, sub, 1)
    has = jnp.max((row_irrep == kinds).astype(jnp.int32), axis=(0, 3)).reshape(chunks, n * N_IRREPS)

    own_a = lambda x: lax.dynamic_slice_in_dim(x, row_pos * tile_a, tile_a, 0)
    own_b = lambda x: lax.dynamic_slice_in_dim(x, col_pos * tile_b, tile_b, 0)
    own_j = lambda x: lax.dynamic_slice_in_dim(x, occ_pos * half, half, 0)
    fixed = (
        occ_irrep, own_a(virt_irrep)[:, None], place_r[:, None], place_c[:, None], own_j(class_c),
        own_a(virt_energy)[:, None], own_b(virt_energy)[None, :], jnp.concatenate([occ_energy, own_j(occ_energy)]),
    )

    def one_round(doubles, cycle, number, base):
        start = number * cap
        local = slot_c - start
        inside = (local >= 0) & (local < cap)
        key = jnp.where(inside, class_c * cap + local, -1)
        right_high, right_low = compact(cycle, key[:, :, None], cap)
        left = sort_rows(doubles, place_r[None, :], n_occ, chunks, n)
        at = lambda x, index: lax.dynamic_index_in_dim(x, index, 0, keepdims=False)
        here = jnp.bitwise_xor(col_pos, row_pos)
        every = [(m, h) for m in range(half) for h in range(chunks)]
        swap = [(d, (d + 1) % n_occ) for d in range(n_occ)]
        spread = exchange(
            lambda t: lax.dynamic_index_in_dim(left, jnp.bitwise_xor(col_pos, t), 2, keepdims=False), "col", n
        )
        spread, right_high, right_low = after(spread, right_high, right_low)

        def to_plane(spread, k):
            m, h = every[k]
            return exchange(lambda t: at(spread[:, m, h], jnp.bitwise_xor(here, t)), "row", n)[None]

        def gather(near):
            bits = 2
            while bits < n:
                near = jnp.concatenate([near, flipped(near, "col", n, bits)])
                bits *= 2
            return near

        def multiply(k, near, far, right, which):
            m, h = every[k]
            scalars = jnp.stack([which, row_pos, col_pos, occ_irrep[which * half + m]]).astype(jnp.int32)
            scalars = jnp.concatenate([scalars, has[h]])
            return product(scalars, row_irrep[:, h], near, far, *right, cap)

        live = {"spread": spread, "right": (right_high, right_low)}
        for step in range(len(every) + 3):
            new = dict(live)
            for stage in range(4):
                k = step - stage
                if not 0 <= k < len(every):
                    continue
                if stage == 0:
                    new["near", k] = to_plane(live["spread"], k)
                elif stage == 1:
                    new["full", k] = gather(live["near", k])
                    del new["near", k]
                elif stage == 2:
                    left_rows = live["full", k], flipped(live["full", k], "col", n, 1)
                    new["got", k] = lax.ppermute(multiply(k, *left_rows, live["right"], 1 - occ_pos), "occ", swap)
                    new["kept", k] = multiply(k, *left_rows, live["right"], occ_pos)
                    del new["full", k]
                else:
                    total = (live["kept", k] + live["got", k]).reshape(n, n * sub, cap)
                    new["part", k] = lax.psum_scatter(total, "row", scatter_dimension=0, tiled=True)[0]
                    del new["kept", k], new["got", k]
            if step == len(every) - 1:
                del new["spread"]
            names = list(new)
            live = dict(zip(names, lax.optimization_barrier(tuple(new[name] for name in names))))
        own = jnp.concatenate([live["part", k] for k in range(len(every))], axis=0).reshape(half, tile_a, cap)
        swapped = lax.ppermute(own, "occ", swap)
        turned = turn(own.reshape(half, n, tile_a // n, cap).transpose(1, 0, 2, 3), n).transpose(1, 0, 2, 3)
        turned = turned.reshape(half, tile_a, cap)
        tables = (occ_pos.reshape(1), own_j(local), (slot_r - start)[:, :, None]) + fixed
        shape = (n_i, tile_a, half, tile_b)
        return finish(tables, own, swapped, turned, base, cap, shape)

    first = one_round(doubles, cycle, jnp.int32(0), None)

    def more(state):
        number, total, doubles, cycle = state
        return number + 1, one_round(doubles, cycle, number, total), doubles, cycle

    state = (jnp.int32(1), first, doubles, cycle)
    return lax.while_loop(lambda state: state[0] < rounds, more, state)[1]


def solution(mesh):
    return jax.shard_map(
        shards,
        mesh=mesh,
        in_specs=(P(None, "row", "occ", "col"), P("occ", "row", None, "col"), P(), P(), P()),
        out_specs=P(None, "row", "occ", "col"),
        check_vma=False,
    )
```

```python
import functools

import jax
import jax.numpy as jnp
from jax import lax
from jax.experimental import pallas as pl
from jax.experimental.pallas import tpu as pltpu
from jax.sharding import PartitionSpec as P

N_IRREPS = 4
VMEM_LIMIT = 56 * 1024 * 1024


def split(x):
    high = x.astype(jnp.bfloat16)
    low = (x - high.astype(jnp.float32)).astype(jnp.bfloat16)
    return high, low


def dot(a, b, contract=((1,), (0,))):
    return lax.dot_general(a, b, (contract, ((), ())), preferred_element_type=jnp.float32)


def sort_body(place_ref, rows_ref, out_ref):
    tile_a, depth = rows_ref.shape[1:]
    chunks, n_piece, _, sub, _ = out_ref.shape[1:]
    places = lax.broadcasted_iota(jnp.int32, (tile_a, tile_a), 0)
    order = (place_ref[...] == places).astype(jnp.float32).astype(jnp.bfloat16)
    high, low = split(rows_ref[0])
    value = dot(order, high) + dot(order, low)
    out_ref[0, :, :, 0] = value.reshape(chunks, n_piece, sub, depth)


def sort_rows(doubles, place, n_occ, chunks, n):
    n_i, tile_a, k_half, tile_c = doubles.shape
    half, sub = n_i // n_occ, tile_a // (chunks * n)
    shape = (half, chunks, n, n_occ, sub, k_half * tile_c)
    return pl.pallas_call(
        sort_body,
        out_shape=jax.ShapeDtypeStruct(shape, jnp.float32),
        grid=(half, n_occ),
        in_specs=[
            pl.BlockSpec((1, tile_a), lambda m, o: (0, 0)),
            pl.BlockSpec((1, tile_a, k_half * tile_c), lambda m, o: (o * half + m, 0, 0)),
        ],
        out_specs=pl.BlockSpec((1, chunks, n, 1, sub, k_half * tile_c), lambda m, o: (m, 0, 0, o, 0, 0)),
        compiler_params=pltpu.CompilerParams(vmem_limit_bytes=VMEM_LIMIT),
        cost_estimate=pl.CostEstimate(
            flops=4 * doubles.size * tile_a, bytes_accessed=8 * doubles.size, transcendentals=0
        ),
    )(place, doubles.reshape(n_i, tile_a, k_half * tile_c))


def compact_body(cap, key_ref, right_ref, high_ref, low_ref, select_ref, both_ref):
    n_j, tile_b = select_ref.shape[:2]
    width = N_IRREPS * cap

    @pl.when(pl.program_id(0) == 0)
    def _():
        for j in range(n_j):
            slots = lax.broadcasted_iota(jnp.int32, (tile_b, width), 1)
            select_ref[j] = (key_ref[j] == slots).astype(jnp.float32).astype(jnp.bfloat16)

    rows = right_ref.shape[0]
    for j in range(n_j):
        high, low = split(right_ref[:, j * tile_b : (j + 1) * tile_b])
        both_ref[j, :rows] = high
        both_ref[j, rows:] = low

    @pl.loop(0, N_IRREPS)
    def _(q):
        span = pl.ds(pl.multiple_of(q * cap, 128), cap)
        total = dot(both_ref[0], select_ref[0, :, span])
        for j in range(1, n_j):
            total += dot(both_ref[j], select_ref[j, :, span])
        high_ref[:, span] = total[:rows].astype(jnp.bfloat16)
        low_ref[:, span] = total[rows:].astype(jnp.bfloat16)


def compact(right, key, cap):
    k_half, tile_c, n_j, tile_b = right.shape
    step = min(tile_c, 256)
    width = N_IRREPS * cap
    out = jax.ShapeDtypeStruct((k_half * tile_c, width), jnp.bfloat16)
    return pl.pallas_call(
        functools.partial(compact_body, cap),
        out_shape=(out, out),
        grid=(k_half * tile_c // step,),
        in_specs=[
            pl.BlockSpec((n_j, tile_b, 1), lambda s: (0, 0, 0)),
            pl.BlockSpec((step, n_j * tile_b), lambda s: (s, 0)),
        ],
        out_specs=[pl.BlockSpec((step, width), lambda s: (s, 0))] * 2,
        scratch_shapes=[
            pltpu.VMEM((n_j, tile_b, width), jnp.bfloat16),
            pltpu.VMEM((n_j, 2 * step, tile_b), jnp.bfloat16),
        ],
        compiler_params=pltpu.CompilerParams(vmem_limit_bytes=VMEM_LIMIT),
        cost_estimate=pl.CostEstimate(
            flops=4 * k_half * tile_c * n_j * tile_b * width, bytes_accessed=4 * right.size, transcendentals=0
        ),
    )(key, right.reshape(k_half * tile_c, n_j * tile_b))


def product_body(cap, scalar_ref, irrep_ref, near_ref, far_ref, high_ref, low_ref, out_ref, *scratch):
    (both_ref,) = scratch
    n_row, _, sub, depth = near_ref.shape[1:]
    rows = n_row * sub
    row_pos, col_pos, row_i = scalar_ref[1], scalar_ref[2], scalar_ref[3]
    for at, ref in enumerate((near_ref, far_ref)):
        high, low = split(ref[0, :, 0].reshape(rows, depth))
        both_ref[at, :rows] = high
        both_ref[at, rows:] = low
    out_ref[...] = jnp.zeros_like(out_ref)

    @pl.loop(0, 2 * N_IRREPS)
    def _(step):
        at, irrep = step // N_IRREPS, step % N_IRREPS
        place = jnp.bitwise_xor(col_pos, at) % 2
        piece = jnp.bitwise_xor(col_pos, 2 * pl.program_id(0) + at)

        @pl.when(scalar_ref[4 + piece * N_IRREPS + irrep] > 0)
        def _():
            span = pl.ds(pl.multiple_of(jnp.bitwise_xor(irrep, row_i) * cap, 128), cap)
            value = dot(both_ref[at], high_ref[:, span])
            value = value[rows:] + dot(both_ref[at, :rows], low_ref[:, span]) + value[:rows]
            for t in range(n_row):
                r = jnp.bitwise_xor(row_pos, t)
                part = value[t * sub : (t + 1) * sub]
                out_ref[r, place] = jnp.where(irrep_ref[r, place] == irrep, part, out_ref[r, place])


def product(scalars, row_irrep, near, far, right_high, right_low, cap):
    n_pair, n_row, _, sub, depth = near.shape
    width = right_high.shape[1]
    pair = lambda v, scalars: (0, jnp.bitwise_xor(scalars[2] // 2, v), 0, 0)
    left = pl.BlockSpec((1, n_row, 1, sub, depth), lambda v, scalars: (v, 0, scalars[0], 0, 0))
    right = pl.BlockSpec((depth, width), lambda v, scalars: (0, 0), pipeline_mode=pl.Buffered(1))
    spec = pltpu.PrefetchScalarGridSpec(
        num_scalar_prefetch=1,
        grid=(n_pair,),
        in_specs=[pl.BlockSpec((n_row, 2, sub, 1), pair), left, left, right, right],
        out_specs=pl.BlockSpec((n_row, 2, sub, cap), pair),
        scratch_shapes=[pltpu.VMEM((2, 2 * n_row * sub, depth), jnp.bfloat16)],
    )
    rows = 2 * n_pair * n_row * sub
    return pl.pallas_call(
        functools.partial(product_body, cap),
        out_shape=jax.ShapeDtypeStruct((n_row, 2 * n_pair, sub, cap), jnp.float32),
        grid_spec=spec,
        compiler_params=pltpu.CompilerParams(vmem_limit_bytes=VMEM_LIMIT),
        cost_estimate=pl.CostEstimate(
            flops=3 * rows * depth * width, bytes_accessed=4 * rows * depth + 4 * depth * width, transcendentals=0
        ),
    )(scalars, row_irrep, near, far, right_high, right_low)


def finish_body(
    cap, occ_pos_ref, key_c_ref, slot_r_ref, irrep_i_ref, irrep_a_ref, place_a_ref, place_b_ref, irrep_jb_ref,
    energy_a_ref, energy_b_ref, energy_ij_ref, own_ref, swapped_ref, turned_ref, *refs,
):
    base_ref = refs[0] if len(refs) == 5 else None
    out_ref, expand_ref, turned_high_ref, turned_low_ref = refs[-4:]
    i = pl.program_id(0)
    half, tile_b = key_c_ref.shape
    tile_a = own_ref.shape[1]
    rows = out_ref.shape[1]

    def one_hot(column, length):
        hit = column == lax.broadcasted_iota(jnp.int32, (column.shape[0], length), 1)
        return hit.astype(jnp.float32).astype(jnp.bfloat16)

    @pl.when((i == 0) & (pl.program_id(1) == 0))
    def _():
        unsort = one_hot(place_b_ref[...], tile_b)
        slots = lax.broadcasted_iota(jnp.int32, (cap, tile_b), 0)
        for j in range(half):
            span = pl.ds(j * tile_b, tile_b)
            hit = key_c_ref[pl.ds(j, 1), :] == slots
            expand_ref[:, span] = hit.astype(jnp.float32).astype(jnp.bfloat16)
            high, low = split(turned_ref[j])
            turned_high_ref[span, :] = dot(unsort, high).astype(jnp.bfloat16)
            turned_low_ref[span, :] = dot(unsort, low).astype(jnp.bfloat16)

    mine = i // half == occ_pos_ref[0]
    unsort = one_hot(place_a_ref[...], tile_a)
    high, low = split(jnp.where(mine, own_ref[0], swapped_ref[0]))
    high, low = dot(unsort, high).astype(jnp.bfloat16), dot(unsort, low).astype(jnp.bfloat16)
    direct = dot(high, expand_ref[...]) + dot(low, expand_ref[...])
    pick = one_hot(slot_r_ref[0], cap)
    across = ((1,), (1,))
    turned = dot(pick, turned_high_ref[...], across) + dot(pick, turned_low_ref[...], across)
    paired = direct + turned
    row_class = jnp.bitwise_xor(irrep_a_ref[...], irrep_i_ref[i])
    for j in range(half):
        piece = paired[:, j * tile_b : (j + 1) * tile_b]
        denom = energy_a_ref[...] + energy_b_ref[...] - energy_ij_ref[i] - energy_ij_ref[2 * half + j]
        value = jnp.where(row_class == irrep_jb_ref[pl.ds(j, 1), :], piece / denom, jnp.zeros_like(piece))
        if base_ref is not None:
            value = value + base_ref[0, :, j, :]
        out_ref[0, :, j, :] = value


def finish(tables, own, swapped, turned, base, cap, shape):
    n_i, tile_a, half, tile_b = shape
    rows = min(tile_a, 256)
    block = pl.BlockSpec((1, rows, half, tile_b), lambda i, s: (i, s, 0, 0))
    part = pl.BlockSpec((1, tile_a, cap), lambda i, s: (i % half, 0, 0))
    smem = pl.BlockSpec(memory_space=pltpu.SMEM)
    whole = lambda x: pl.BlockSpec(x.shape, lambda i, s: (0,) * x.ndim)
    column = pl.BlockSpec((rows, 1), lambda i, s: (s, 0))
    occ_pos, key_c, slot_r, irrep_i, irrep_a, place_a, place_b, irrep_jb, energy_a, energy_b, energy_ij = tables
    args = list(tables) + [own, swapped, turned]
    specs = [
        smem, whole(key_c), pl.BlockSpec((1, rows, 1), lambda i, s: (i, s, 0)), smem, column, column, whole(place_b),
        whole(irrep_jb), column, whole(energy_b), smem, part, part, whole(turned),
    ]
    aliases = {}
    if base is not None:
        aliases = {len(args): 0}
        args.append(base)
        specs.append(block)
    return pl.pallas_call(
        functools.partial(finish_body, cap),
        out_shape=jax.ShapeDtypeStruct(shape, jnp.float32),
        grid=(n_i, tile_a // rows),
        in_specs=specs,
        out_specs=block,
        scratch_shapes=[
            pltpu.VMEM((cap, half * tile_b), jnp.bfloat16),
            pltpu.VMEM((half * tile_b, cap), jnp.bfloat16),
            pltpu.VMEM((half * tile_b, cap), jnp.bfloat16),
        ],
        input_output_aliases=aliases,
        compiler_params=pltpu.CompilerParams(vmem_limit_bytes=VMEM_LIMIT),
        cost_estimate=pl.CostEstimate(
            flops=8 * n_i * tile_a * cap * half * tile_b, bytes_accessed=4 * n_i * tile_a * (half * tile_b + cap),
            transcendentals=0,
        ),
    )(*args)


def after(x, *others):
    return lax.optimization_barrier((x,) + others)


def flipped(x, axis, n, bits):
    return lax.ppermute(x, axis, [(d, d ^ bits) for d in range(n)])


def exchange(pick, axis, n):
    return jnp.stack([pick(0)] + [flipped(pick(t), axis, n, t) for t in range(1, n)])


def spread_out(x, axis):
    return lax.all_to_all(x, axis, split_axis=0, concat_axis=0, tiled=True)


def shards(doubles, cycle, occ_energy, virt_energy, orbital_irrep):
    n_i, tile_a, k_half, tile_c = doubles.shape
    n_j, tile_b = cycle.shape[2:]
    n, n_occ = lax.axis_size("row"), lax.axis_size("occ")
    half = n_j // n_occ
    columns = n_j * tile_b
    cap = min(columns, -(-columns * 5 // (N_IRREPS * 4 * 128)) * 128)
    chunks = 2 if tile_a % (16 * n) == 0 else 1
    sub = tile_a // (chunks * n)
    row_pos, col_pos, occ_pos = lax.axis_index("row"), lax.axis_index("col"), lax.axis_index("occ")
    occ_irrep, virt_irrep = orbital_irrep[:n_j], orbital_irrep[n_j:]

    blocks = virt_irrep.reshape(n, tile_b)
    kinds = jnp.arange(N_IRREPS, dtype=jnp.int32)
    counts = jnp.sum((blocks[:, None, :] == kinds[:, None]).astype(jnp.int32), axis=2)
    sizes = sum(counts[:, jnp.bitwise_xor(kinds, occ_irrep[j])] for j in range(n_j))
    rounds = (jnp.max(sizes) + cap - 1) // cap

    starts = jnp.cumsum(counts, axis=1) - counts

    def places(block_pos):
        irrep = lax.dynamic_index_in_dim(blocks, block_pos, 0, keepdims=False)
        count = lax.dynamic_index_in_dim(counts, block_pos, 0, keepdims=False)
        start = lax.dynamic_index_in_dim(starts, block_pos, 0, keepdims=False)
        order = jnp.arange(tile_b, dtype=jnp.int32)
        earlier = (irrep[:, None] == irrep[None, :]) & (order[:, None] < order[None, :])
        rank = jnp.sum(earlier.astype(jnp.int32), axis=0)
        look_up = lambda table, index: sum(jnp.where(index == g, table[g], 0) for g in range(N_IRREPS))
        slots = []
        for j in range(n_j):
            before = jnp.zeros((tile_b,), jnp.int32)
            for other in range(j):
                before += look_up(count, jnp.bitwise_xor(irrep, jnp.bitwise_xor(occ_irrep[j], occ_irrep[other])))
            slots.append(before + rank)
        return jnp.stack(slots), jnp.bitwise_xor(irrep[None, :], occ_irrep[:, None]), look_up(start, irrep) + rank

    slot_c, class_c, place_c = places(col_pos)
    slot_r, _, place_r = places(row_pos)

    order = jnp.arange(tile_a, dtype=jnp.int32)
    row_irrep = sum((order[None, :] >= starts[:, g, None]).astype(jnp.int32) for g in range(1, N_IRREPS))
    row_irrep = row_irrep.reshape(n, chunks, n, sub, 1)
    has = jnp.max((row_irrep == kinds).astype(jnp.int32), axis=(0, 3)).reshape(chunks, n * N_IRREPS)

    own_a = lambda x: lax.dynamic_slice_in_dim(x, row_pos * tile_a, tile_a, 0)
    own_b = lambda x: lax.dynamic_slice_in_dim(x, col_pos * tile_b, tile_b, 0)
    own_j = lambda x: lax.dynamic_slice_in_dim(x, occ_pos * half, half, 0)
    fixed = (
        occ_irrep, own_a(virt_irrep)[:, None], place_r[:, None], place_c[:, None], own_j(class_c),
        own_a(virt_energy)[:, None], own_b(virt_energy)[None, :], jnp.concatenate([occ_energy, own_j(occ_energy)]),
    )

    def one_round(doubles, cycle, number, base):
        start = number * cap
        local = slot_c - start
        inside = (local >= 0) & (local < cap)
        key = jnp.where(inside, class_c * cap + local, -1)
        right_high, right_low = compact(cycle, key[:, :, None], cap)
        left = sort_rows(doubles, place_r[None, :], n_occ, chunks, n)
        at = lambda x, index: lax.dynamic_index_in_dim(x, index, 0, keepdims=False)
        here = jnp.bitwise_xor(col_pos, row_pos)
        every = [(m, h) for m in range(half) for h in range(chunks)]
        swap = [(d, (d + 1) % n_occ) for d in range(n_occ)]
        spread = exchange(
            lambda t: lax.dynamic_index_in_dim(left, jnp.bitwise_xor(col_pos, t), 2, keepdims=False), "col", n
        )
        spread, right_high, right_low = after(spread, right_high, right_low)

        def to_plane(spread, k):
            m, h = every[k]
            return exchange(lambda t: at(spread[:, m, h], jnp.bitwise_xor(here, t)), "row", n)[None]

        def gather(near):
            bits = 2
            while bits < n:
                near = jnp.concatenate([near, flipped(near, "col", n, bits)])
                bits *= 2
            return near

        def multiply(k, near, far, right, which):
            m, h = every[k]
            scalars = jnp.stack([which, row_pos, col_pos, occ_irrep[which * half + m]]).astype(jnp.int32)
            scalars = jnp.concatenate([scalars, has[h]])
            return product(scalars, row_irrep[:, h], near, far, *right, cap)

        live = {"spread": spread, "right": (right_high, right_low)}
        for step in range(len(every) + 3):
            new = dict(live)
            for stage in range(4):
                k = step - stage
                if not 0 <= k < len(every):
                    continue
                if stage == 0:
                    new["near", k] = to_plane(live["spread"], k)
                elif stage == 1:
                    new["full", k] = gather(live["near", k])
                    del new["near", k]
                elif stage == 2:
                    left_rows = live["full", k], flipped(live["full", k], "col", n, 1)
                    new["got", k] = lax.ppermute(multiply(k, *left_rows, live["right"], 1 - occ_pos), "occ", swap)
                    new["kept", k] = multiply(k, *left_rows, live["right"], occ_pos)
                    del new["full", k]
                else:
                    total = (live["kept", k] + live["got", k]).reshape(n, n * sub, cap)
                    new["part", k] = lax.psum_scatter(total, "row", scatter_dimension=0, tiled=True)[0]
                    del new["kept", k], new["got", k]
            if step == len(every) - 1:
                del new["spread"]
            if step == len(every) + 2:
                first = [live["part", k].reshape(n, 1, sub, cap) for k in range(len(every) - 1)]
                new["turned", 0] = spread_out(jnp.concatenate(first, axis=1), "col")
            names = list(new)
            live = dict(zip(names, lax.optimization_barrier(tuple(new[name] for name in names))))
        own = jnp.concatenate([live["part", k] for k in range(len(every))], axis=0).reshape(half, tile_a, cap)
        swapped = lax.ppermute(own, "occ", swap)
        last = spread_out(live["part", len(every) - 1].reshape(n, 1, sub, cap), "col")
        turned = jnp.concatenate([live["turned", 0], last], axis=1)
        turned = spread_out(spread_out(turned, "row"), "col").transpose(1, 0, 2, 3).reshape(half, tile_a, cap)
        tables = (occ_pos.reshape(1), own_j(local), (slot_r - start)[:, :, None]) + fixed
        shape = (n_i, tile_a, half, tile_b)
        return finish(tables, own, swapped, turned, base, cap, shape)

    first = one_round(doubles, cycle, jnp.int32(0), None)

    def more(state):
        number, total, doubles, cycle = state
        return number + 1, one_round(doubles, cycle, number, total), doubles, cycle

    state = (jnp.int32(1), first, doubles, cycle)
    return lax.while_loop(lambda state: state[0] < rounds, more, state)[1]


def solution(mesh):
    return jax.shard_map(
        shards,
        mesh=mesh,
        in_specs=(P(None, "row", "occ", "col"), P("occ", "row", None, "col"), P(), P(), P()),
        out_specs=P(None, "row", "occ", "col"),
        check_vma=False,
    )
```

```python
import functools

import jax
import jax.numpy as jnp
from jax import lax
from jax.experimental import pallas as pl
from jax.experimental.pallas import tpu as pltpu
from jax.sharding import PartitionSpec as P

N_IRREPS = 4
VMEM_LIMIT = 56 * 1024 * 1024


def split(x):
    high = x.astype(jnp.bfloat16)
    low = (x - high.astype(jnp.float32)).astype(jnp.bfloat16)
    return high, low


def dot(a, b, contract=((1,), (0,))):
    return lax.dot_general(a, b, (contract, ((), ())), preferred_element_type=jnp.float32)


def sort_body(place_ref, rows_ref, out_ref):
    tile_a, depth = rows_ref.shape[1:]
    chunks, n_piece, _, sub, _ = out_ref.shape[1:]
    places = lax.broadcasted_iota(jnp.int32, (tile_a, tile_a), 0)
    order = (place_ref[...] == places).astype(jnp.float32).astype(jnp.bfloat16)
    high, low = split(rows_ref[0])
    value = dot(order, high) + dot(order, low)
    out_ref[0, :, :, 0] = value.reshape(chunks, n_piece, sub, depth)


def sort_rows(doubles, place, n_occ, chunks, n):
    n_i, tile_a, k_half, tile_c = doubles.shape
    half, sub = n_i // n_occ, tile_a // (chunks * n)
    shape = (half, chunks, n, n_occ, sub, k_half * tile_c)
    return pl.pallas_call(
        sort_body,
        out_shape=jax.ShapeDtypeStruct(shape, jnp.float32),
        grid=(half, n_occ),
        in_specs=[
            pl.BlockSpec((1, tile_a), lambda m, o: (0, 0)),
            pl.BlockSpec((1, tile_a, k_half * tile_c), lambda m, o: (o * half + m, 0, 0)),
        ],
        out_specs=pl.BlockSpec((1, chunks, n, 1, sub, k_half * tile_c), lambda m, o: (m, 0, 0, o, 0, 0)),
        compiler_params=pltpu.CompilerParams(vmem_limit_bytes=VMEM_LIMIT),
        cost_estimate=pl.CostEstimate(
            flops=4 * doubles.size * tile_a, bytes_accessed=8 * doubles.size, transcendentals=0
        ),
    )(place, doubles.reshape(n_i, tile_a, k_half * tile_c))


def compact_body(cap, key_ref, right_ref, high_ref, low_ref, select_ref, both_ref):
    n_j, tile_b = select_ref.shape[:2]
    width = N_IRREPS * cap

    @pl.when(pl.program_id(0) == 0)
    def _():
        for j in range(n_j):
            slots = lax.broadcasted_iota(jnp.int32, (tile_b, width), 1)
            select_ref[j] = (key_ref[j] == slots).astype(jnp.float32).astype(jnp.bfloat16)

    rows = right_ref.shape[0]
    for j in range(n_j):
        high, low = split(right_ref[:, j * tile_b : (j + 1) * tile_b])
        both_ref[j, :rows] = high
        both_ref[j, rows:] = low

    @pl.loop(0, N_IRREPS)
    def _(q):
        span = pl.ds(pl.multiple_of(q * cap, 128), cap)
        total = dot(both_ref[0], select_ref[0, :, span])
        for j in range(1, n_j):
            total += dot(both_ref[j], select_ref[j, :, span])
        high_ref[:, span] = total[:rows].astype(jnp.bfloat16)
        low_ref[:, span] = total[rows:].astype(jnp.bfloat16)


def compact(right, key, cap):
    k_half, tile_c, n_j, tile_b = right.shape
    step = min(tile_c, 256)
    width = N_IRREPS * cap
    out = jax.ShapeDtypeStruct((k_half * tile_c, width), jnp.bfloat16)
    return pl.pallas_call(
        functools.partial(compact_body, cap),
        out_shape=(out, out),
        grid=(k_half * tile_c // step,),
        in_specs=[
            pl.BlockSpec((n_j, tile_b, 1), lambda s: (0, 0, 0)),
            pl.BlockSpec((step, n_j * tile_b), lambda s: (s, 0)),
        ],
        out_specs=[pl.BlockSpec((step, width), lambda s: (s, 0))] * 2,
        scratch_shapes=[
            pltpu.VMEM((n_j, tile_b, width), jnp.bfloat16),
            pltpu.VMEM((n_j, 2 * step, tile_b), jnp.bfloat16),
        ],
        compiler_params=pltpu.CompilerParams(vmem_limit_bytes=VMEM_LIMIT),
        cost_estimate=pl.CostEstimate(
            flops=4 * k_half * tile_c * n_j * tile_b * width, bytes_accessed=4 * right.size, transcendentals=0
        ),
    )(key, right.reshape(k_half * tile_c, n_j * tile_b))


def product_body(cap, scalar_ref, irrep_ref, near_ref, far_ref, high_ref, low_ref, out_ref, *scratch):
    (both_ref,) = scratch
    n_row, _, sub, depth = near_ref.shape[1:]
    rows = n_row * sub
    row_pos, col_pos, row_i = scalar_ref[1], scalar_ref[2], scalar_ref[3]
    for at, ref in enumerate((near_ref, far_ref)):
        high, low = split(ref[0, :, 0].reshape(rows, depth))
        both_ref[at, :rows] = high
        both_ref[at, rows:] = low
    out_ref[...] = jnp.zeros_like(out_ref)

    @pl.loop(0, 2 * N_IRREPS)
    def _(step):
        at, irrep = step // N_IRREPS, step % N_IRREPS
        place = jnp.bitwise_xor(col_pos, at) % 2
        piece = jnp.bitwise_xor(col_pos, 2 * pl.program_id(0) + at)

        @pl.when(scalar_ref[4 + piece * N_IRREPS + irrep] > 0)
        def _():
            span = pl.ds(pl.multiple_of(jnp.bitwise_xor(irrep, row_i) * cap, 128), cap)
            value = dot(both_ref[at], high_ref[:, span])
            value = value[rows:] + dot(both_ref[at, :rows], low_ref[:, span]) + value[:rows]
            for t in range(n_row):
                r = jnp.bitwise_xor(row_pos, t)
                part = value[t * sub : (t + 1) * sub]
                out_ref[r, place] = jnp.where(irrep_ref[r, place] == irrep, part, out_ref[r, place])


def product(scalars, row_irrep, near, far, right_high, right_low, cap):
    n_pair, n_row, _, sub, depth = near.shape
    width = right_high.shape[1]
    pair = lambda v, scalars: (0, jnp.bitwise_xor(scalars[2] // 2, v), 0, 0)
    left = pl.BlockSpec((1, n_row, 1, sub, depth), lambda v, scalars: (v, 0, scalars[0], 0, 0))
    right = pl.BlockSpec((depth, width), lambda v, scalars: (0, 0), pipeline_mode=pl.Buffered(1))
    spec = pltpu.PrefetchScalarGridSpec(
        num_scalar_prefetch=1,
        grid=(n_pair,),
        in_specs=[pl.BlockSpec((n_row, 2, sub, 1), pair), left, left, right, right],
        out_specs=pl.BlockSpec((n_row, 2, sub, cap), pair),
        scratch_shapes=[pltpu.VMEM((2, 2 * n_row * sub, depth), jnp.bfloat16)],
    )
    rows = 2 * n_pair * n_row * sub
    return pl.pallas_call(
        functools.partial(product_body, cap),
        out_shape=jax.ShapeDtypeStruct((n_row, 2 * n_pair, sub, cap), jnp.float32),
        grid_spec=spec,
        compiler_params=pltpu.CompilerParams(vmem_limit_bytes=VMEM_LIMIT),
        cost_estimate=pl.CostEstimate(
            flops=3 * rows * depth * width, bytes_accessed=4 * rows * depth + 4 * depth * width, transcendentals=0
        ),
    )(scalars, row_irrep, near, far, right_high, right_low)


def finish_body(
    cap, occ_pos_ref, key_c_ref, slot_r_ref, irrep_i_ref, irrep_a_ref, place_a_ref, place_b_ref, irrep_jb_ref,
    energy_a_ref, energy_b_ref, energy_ij_ref, own_ref, swapped_ref, turned_ref, *refs,
):
    base_ref = refs[0] if len(refs) == 5 else None
    out_ref, expand_ref, turned_high_ref, turned_low_ref = refs[-4:]
    i = pl.program_id(0)
    half, tile_b = key_c_ref.shape
    tile_a = own_ref.shape[1]
    rows = out_ref.shape[1]

    def one_hot(column, length):
        hit = column == lax.broadcasted_iota(jnp.int32, (column.shape[0], length), 1)
        return hit.astype(jnp.float32).astype(jnp.bfloat16)

    @pl.when((i == 0) & (pl.program_id(1) == 0))
    def _():
        unsort = one_hot(place_b_ref[...], tile_b)
        slots = lax.broadcasted_iota(jnp.int32, (cap, tile_b), 0)
        for j in range(half):
            span = pl.ds(j * tile_b, tile_b)
            hit = key_c_ref[pl.ds(j, 1), :] == slots
            expand_ref[:, span] = hit.astype(jnp.float32).astype(jnp.bfloat16)
            high, low = split(turned_ref[j])
            turned_high_ref[span, :] = dot(unsort, high).astype(jnp.bfloat16)
            turned_low_ref[span, :] = dot(unsort, low).astype(jnp.bfloat16)

    mine = i // half == occ_pos_ref[0]
    unsort = one_hot(place_a_ref[...], tile_a)
    high, low = split(jnp.where(mine, own_ref[0], swapped_ref[0]))
    high, low = dot(unsort, high).astype(jnp.bfloat16), dot(unsort, low).astype(jnp.bfloat16)
    direct = dot(high, expand_ref[...]) + dot(low, expand_ref[...])
    pick = one_hot(slot_r_ref[0], cap)
    across = ((1,), (1,))
    turned = dot(pick, turned_high_ref[...], across) + dot(pick, turned_low_ref[...], across)
    paired = direct + turned
    row_class = jnp.bitwise_xor(irrep_a_ref[...], irrep_i_ref[i])
    for j in range(half):
        piece = paired[:, j * tile_b : (j + 1) * tile_b]
        denom = energy_a_ref[...] + energy_b_ref[...] - energy_ij_ref[i] - energy_ij_ref[2 * half + j]
        value = jnp.where(row_class == irrep_jb_ref[pl.ds(j, 1), :], piece / denom, jnp.zeros_like(piece))
        if base_ref is not None:
            value = value + base_ref[0, :, j, :]
        out_ref[0, :, j, :] = value


def finish(tables, own, swapped, turned, base, cap, shape):
    n_i, tile_a, half, tile_b = shape
    rows = min(tile_a, 512)
    block = pl.BlockSpec((1, rows, half, tile_b), lambda i, s: (i, s, 0, 0))
    part = pl.BlockSpec((1, tile_a, cap), lambda i, s: (i % half, 0, 0))
    smem = pl.BlockSpec(memory_space=pltpu.SMEM)
    whole = lambda x: pl.BlockSpec(x.shape, lambda i, s: (0,) * x.ndim)
    column = pl.BlockSpec((rows, 1), lambda i, s: (s, 0))
    occ_pos, key_c, slot_r, irrep_i, irrep_a, place_a, place_b, irrep_jb, energy_a, energy_b, energy_ij = tables
    args = list(tables) + [own, swapped, turned]
    specs = [
        smem, whole(key_c), pl.BlockSpec((1, rows, 1), lambda i, s: (i, s, 0)), smem, column, column, whole(place_b),
        whole(irrep_jb), column, whole(energy_b), smem, part, part, whole(turned),
    ]
    aliases = {}
    if base is not None:
        aliases = {len(args): 0}
        args.append(base)
        specs.append(block)
    return pl.pallas_call(
        functools.partial(finish_body, cap),
        out_shape=jax.ShapeDtypeStruct(shape, jnp.float32),
        grid=(n_i, tile_a // rows),
        in_specs=specs,
        out_specs=block,
        scratch_shapes=[
            pltpu.VMEM((cap, half * tile_b), jnp.bfloat16),
            pltpu.VMEM((half * tile_b, cap), jnp.bfloat16),
            pltpu.VMEM((half * tile_b, cap), jnp.bfloat16),
        ],
        input_output_aliases=aliases,
        compiler_params=pltpu.CompilerParams(vmem_limit_bytes=VMEM_LIMIT),
        cost_estimate=pl.CostEstimate(
            flops=8 * n_i * tile_a * cap * half * tile_b, bytes_accessed=4 * n_i * tile_a * (half * tile_b + cap),
            transcendentals=0,
        ),
    )(*args)


def after(x, *others):
    return lax.optimization_barrier((x,) + others)


def flipped(x, axis, n, bits):
    return lax.ppermute(x, axis, [(d, d ^ bits) for d in range(n)])


def exchange(pick, axis, n):
    return jnp.stack([pick(0)] + [flipped(pick(t), axis, n, t) for t in range(1, n)])


def spread_out(x, axis):
    return lax.all_to_all(x, axis, split_axis=0, concat_axis=0, tiled=True)


def shards(doubles, cycle, occ_energy, virt_energy, orbital_irrep):
    n_i, tile_a, k_half, tile_c = doubles.shape
    n_j, tile_b = cycle.shape[2:]
    n, n_occ = lax.axis_size("row"), lax.axis_size("occ")
    half = n_j // n_occ
    columns = n_j * tile_b
    cap = min(columns, -(-columns * 5 // (N_IRREPS * 4 * 128)) * 128)
    chunks = 2 if tile_a % (16 * n) == 0 else 1
    sub = tile_a // (chunks * n)
    row_pos, col_pos, occ_pos = lax.axis_index("row"), lax.axis_index("col"), lax.axis_index("occ")
    occ_irrep, virt_irrep = orbital_irrep[:n_j], orbital_irrep[n_j:]

    blocks = virt_irrep.reshape(n, tile_b)
    kinds = jnp.arange(N_IRREPS, dtype=jnp.int32)
    counts = jnp.sum((blocks[:, None, :] == kinds[:, None]).astype(jnp.int32), axis=2)
    sizes = sum(counts[:, jnp.bitwise_xor(kinds, occ_irrep[j])] for j in range(n_j))
    rounds = (jnp.max(sizes) + cap - 1) // cap

    starts = jnp.cumsum(counts, axis=1) - counts

    def places(block_pos):
        irrep = lax.dynamic_index_in_dim(blocks, block_pos, 0, keepdims=False)
        count = lax.dynamic_index_in_dim(counts, block_pos, 0, keepdims=False)
        start = lax.dynamic_index_in_dim(starts, block_pos, 0, keepdims=False)
        order = jnp.arange(tile_b, dtype=jnp.int32)
        earlier = (irrep[:, None] == irrep[None, :]) & (order[:, None] < order[None, :])
        rank = jnp.sum(earlier.astype(jnp.int32), axis=0)
        look_up = lambda table, index: sum(jnp.where(index == g, table[g], 0) for g in range(N_IRREPS))
        slots = []
        for j in range(n_j):
            before = jnp.zeros((tile_b,), jnp.int32)
            for other in range(j):
                before += look_up(count, jnp.bitwise_xor(irrep, jnp.bitwise_xor(occ_irrep[j], occ_irrep[other])))
            slots.append(before + rank)
        return jnp.stack(slots), jnp.bitwise_xor(irrep[None, :], occ_irrep[:, None]), look_up(start, irrep) + rank

    slot_c, class_c, place_c = places(col_pos)
    slot_r, _, place_r = places(row_pos)

    order = jnp.arange(tile_a, dtype=jnp.int32)
    row_irrep = sum((order[None, :] >= starts[:, g, None]).astype(jnp.int32) for g in range(1, N_IRREPS))
    row_irrep = row_irrep.reshape(n, chunks, n, sub, 1)
    has = jnp.max((row_irrep == kinds).astype(jnp.int32), axis=(0, 3)).reshape(chunks, n * N_IRREPS)

    own_a = lambda x: lax.dynamic_slice_in_dim(x, row_pos * tile_a, tile_a, 0)
    own_b = lambda x: lax.dynamic_slice_in_dim(x, col_pos * tile_b, tile_b, 0)
    own_j = lambda x: lax.dynamic_slice_in_dim(x, occ_pos * half, half, 0)
    fixed = (
        occ_irrep, own_a(virt_irrep)[:, None], place_r[:, None], place_c[:, None], own_j(class_c),
        own_a(virt_energy)[:, None], own_b(virt_energy)[None, :], jnp.concatenate([occ_energy, own_j(occ_energy)]),
    )

    def one_round(doubles, cycle, number, base):
        start = number * cap
        local = slot_c - start
        inside = (local >= 0) & (local < cap)
        key = jnp.where(inside, class_c * cap + local, -1)
        right_high, right_low = compact(cycle, key[:, :, None], cap)
        left = sort_rows(doubles, place_r[None, :], n_occ, chunks, n)
        at = lambda x, index: lax.dynamic_index_in_dim(x, index, 0, keepdims=False)
        here = jnp.bitwise_xor(col_pos, row_pos)
        every = [(m, h) for m in range(half) for h in range(chunks)]
        swap = [(d, (d + 1) % n_occ) for d in range(n_occ)]
        spread = exchange(
            lambda t: lax.dynamic_index_in_dim(left, jnp.bitwise_xor(col_pos, t), 2, keepdims=False), "col", n
        )
        spread, right_high, right_low = after(spread, right_high, right_low)

        def to_plane(spread, k):
            m, h = every[k]
            return exchange(lambda t: at(spread[:, m, h], jnp.bitwise_xor(here, t)), "row", n)[None]

        def gather(near):
            bits = 2
            while bits < n:
                near = jnp.concatenate([near, flipped(near, "col", n, bits)])
                bits *= 2
            return near

        def multiply(k, near, far, right, which):
            m, h = every[k]
            scalars = jnp.stack([which, row_pos, col_pos, occ_irrep[which * half + m]]).astype(jnp.int32)
            scalars = jnp.concatenate([scalars, has[h]])
            return product(scalars, row_irrep[:, h], near, far, *right, cap)

        live = {"spread": spread, "right": (right_high, right_low)}
        for step in range(len(every) + 3):
            new = dict(live)
            for stage in range(5):
                k = step - stage
                if not 0 <= k < len(every):
                    continue
                wait = int(k == 0 and len(every) > 2)
                if stage == 0:
                    new["near", k] = to_plane(live["spread"], k)
                elif stage == 1:
                    new["full", k] = gather(live["near", k])
                    del new["near", k]
                elif stage == 2:
                    left_rows = live["full", k], flipped(live["full", k], "col", n, 1)
                    new["got", k] = lax.ppermute(multiply(k, *left_rows, live["right"], 1 - occ_pos), "occ", swap)
                    if wait:
                        new["rows", k] = left_rows
                    else:
                        new["kept", k] = multiply(k, *left_rows, live["right"], occ_pos)
                    del new["full", k]
                elif stage == 3 and wait:
                    new["kept", k] = multiply(k, *live["rows", k], live["right"], occ_pos)
                    del new["rows", k]
                elif stage == 3 + wait:
                    total = (live["kept", k] + live["got", k]).reshape(n, n * sub, cap)
                    new["part", k] = lax.psum_scatter(total, "row", scatter_dimension=0, tiled=True)[0]
                    del new["kept", k], new["got", k]
            if step == len(every) - 1:
                del new["spread"]
            if step == len(every) + 2:
                first = [live["part", k].reshape(n, 1, sub, cap) for k in range(len(every) - 1)]
                new["turned", 0] = spread_out(jnp.concatenate(first, axis=1), "col")
            names = list(new)
            live = dict(zip(names, lax.optimization_barrier(tuple(new[name] for name in names))))
        own = jnp.concatenate([live["part", k] for k in range(len(every))], axis=0).reshape(half, tile_a, cap)
        swapped = lax.ppermute(own, "occ", swap)
        last = spread_out(live["part", len(every) - 1].reshape(n, 1, sub, cap), "col")
        turned = jnp.concatenate([live["turned", 0], last], axis=1)
        turned = spread_out(spread_out(turned, "row"), "col").transpose(1, 0, 2, 3).reshape(half, tile_a, cap)
        tables = (occ_pos.reshape(1), own_j(local), (slot_r - start)[:, :, None]) + fixed
        shape = (n_i, tile_a, half, tile_b)
        return finish(tables, own, swapped, turned, base, cap, shape)

    first = one_round(doubles, cycle, jnp.int32(0), None)

    def more(state):
        number, total, doubles, cycle = state
        return number + 1, one_round(doubles, cycle, number, total), doubles, cycle

    state = (jnp.int32(1), first, doubles, cycle)
    return lax.while_loop(lambda state: state[0] < rounds, more, state)[1]


def solution(mesh):
    return jax.shard_map(
        shards,
        mesh=mesh,
        in_specs=(P(None, "row", "occ", "col"), P("occ", "row", None, "col"), P(), P(), P()),
        out_specs=P(None, "row", "occ", "col"),
        check_vma=False,
    )
```
